256 devices in a mesh: dp: 32 (over x, z_hi, core), space: 8 (over y, z_lo).
Axes of the slice: x: 4, y: 4, z: 8 (z_hi: 4, z_lo: 2; z = z_hi * 2 + z_lo), core: 2. Of those that a mesh axis runs over, the one named last changes fastest.
Arguments:
- layer_input: bfloat16 [32, 32, 16, 16, 128], P('dp', None, 'space'), may hold values from -6 to 6
- pre_act: bfloat16 [32, 32, 16, 16, 128], P('dp', None, 'space'), may hold values from -6 to 6
- cotangent: bfloat16 [32, 32, 16, 16, 128], P('dp', None, 'space'), may hold values from -6 to 6
- weight_one: bfloat16 [3, 3, 3, 32, 32], replicated, may hold values from -0.21875 to 0.21875
- weight_two: bfloat16 [3, 3, 3, 32, 32], replicated, may hold values from -0.21875 to 0.21875
Outputs:
- grad_input: bfloat16 [32, 32, 16, 16, 128], P('dp', None, 'space')
- grad_one: float32 [3, 3, 3, 32, 32], replicated
- grad_two: float32 [3, 3, 3, 32, 32], replicated
The draws below stay inside these ranges and needn't reach their ends.
All inputs are finite; a program needn't handle non-finite values.
Results may differ from the reference program's by a relative error of at most 0.0049.
Values may be sent and summed in bfloat16 or wider, within the bound.
A program may use at most 64 MiB of HBM per device.

```python
import jax
import jax.numpy as jnp
from jax import lax

CH = 32
KS = 3
HGT = 16
WID = 128
GROUPS = 32
DEPTH = 16


def block_levels(own_key, extent, split, smallest, largest):
    def one(position, blocks):
        steps = jax.random.uniform(jax.random.fold_in(jax.random.fold_in(own_key, 6), position), (blocks,), jnp.float32, smallest / len(split), largest / len(split))
        return jnp.repeat(jnp.exp(steps), extent[position] // blocks).reshape((-1,) + (1,) * (len(extent) - position - 1))

    loudness = one(*split[0])
    for cut in split[1:]:
        loudness = loudness * one(*cut)
    return loudness


def gaussian(stream_key, shape, scale, most, shards=(), kind=jnp.bfloat16):
    entries = jax.random.normal(stream_key, shape, jnp.float32) * scale
    if len(shards) > 0:
        entries = block_levels(stream_key, shape, shards, -0.22, 0.18) * entries
    return jnp.clip(entries, min=-most, max=most).astype(kind)


def setup_inputs(seed: int = 0) -> dict:
    seeds = jax.random.split(jax.random.key(seed), 6)
    return {
        "layer_input": gaussian(seeds[0], (GROUPS, CH, DEPTH, HGT, WID), 1.0, 6.0, ((0, 32), (2, 8))),
        "pre_act": gaussian(seeds[1], (GROUPS, CH, DEPTH, HGT, WID), 1.0, 6.0, ((0, 32), (2, 8))),
        "cotangent": gaussian(seeds[2], (GROUPS, CH, DEPTH, HGT, WID), 1.0, 6.0, ((0, 32), (2, 8))),
        "weight_one": gaussian(seeds[3], (KS, KS, KS, CH, CH), (KS * KS * KS * CH) ** -0.5, 0.21875),
        "weight_two": gaussian(seeds[4], (KS, KS, KS, CH, CH), (KS * KS * KS * CH) ** -0.5, 0.21875),
    }


def leaky(value):
    return jnp.where(value > 0, value, 0.3 * value)

def pad_all(value):
    return jnp.pad(value, ((0, 0), (1, 1), (1, 1), (1, 1)))

def kernel_grad(top, low_pad):
    depth, height, width = (top.shape[1], top.shape[2], top.shape[3])
    rows = []
    for kd in range(3):
        for kh in range(3):
            for kw in range(3):
                window = low_pad[:, kd:kd + depth, kh:kh + height, kw:kw + width]
                rows.append(jnp.einsum('odhw,idhw->oi', top, window, precision=lax.Precision.HIGHEST))
    return jnp.stack(rows).reshape(3, 3, 3, top.shape[0], low_pad.shape[0])

def transposed(top_pad, weight, depth):
    height, width = (top_pad.shape[2] - 2, top_pad.shape[3] - 2)
    total = jnp.zeros((weight.shape[4], depth, height, width), jnp.float32)
    for kd in range(3):
        for kh in range(3):
            for kw in range(3):
                window = top_pad[:, 2 - kd:2 - kd + depth, 2 - kh:2 - kh + height, 2 - kw:2 - kw + width]
                total = total + jnp.einsum('oi,odhw->idhw', weight[kd, kh, kw], window, precision=lax.Precision.HIGHEST)
    return total

def reference(layer_input, pre_act, cotangent, weight_one, weight_two):
    wone = weight_one.astype(jnp.float32)
    wtwo = weight_two.astype(jnp.float32)
    depth = layer_input.shape[2]

    def one_sample(carry, sample):
        source, pre, cot = sample
        activation = leaky(pre.astype(jnp.float32)).astype(jnp.bfloat16)
        cot32 = cot.astype(jnp.float32)
        gtwo = kernel_grad(cot32, pad_all(activation.astype(jnp.float32)))
        grad_act = transposed(pad_all(cot32), wtwo, depth)
        grad_pre = (grad_act * jnp.where(pre > 0, 1.0, 0.3)).astype(jnp.bfloat16)
        gp32 = grad_pre.astype(jnp.float32)
        gone = kernel_grad(gp32, pad_all(source.astype(jnp.float32)))
        grad_in = transposed(pad_all(gp32), wone, depth).astype(jnp.bfloat16)
        return ((carry[0] + gone, carry[1] + gtwo), grad_in)
    zeros = jnp.zeros(weight_one.shape, jnp.float32)
    sums, grad_input = lax.scan(one_sample, (zeros, zeros), (layer_input, pre_act, cotangent))
    scale = (layer_input.shape[0] * depth * layer_input.shape[3] * layer_input.shape[4]) ** (-0.5)
    return (grad_input, sums[0] * scale, sums[1] * scale)
```

```python
import functools

import jax
import jax.numpy as jnp
from jax import lax
from jax.experimental import pallas as pl
from jax.experimental.pallas import tpu as pltpu
from jax.sharding import PartitionSpec as P

CH = 32
HGT = 16
WID = 128
PLANE = HGT * WID
TILES = 32
USED = 27
F32 = jnp.float32
BF16 = jnp.bfloat16


def leaky(value):
    return jnp.where(value > 0, value, 0.3 * value)


def kernel(
    cfg,
    src_hbm, pre_hbm, cot_hbm, w1_ref, w2_ref,
    gin_hbm, g1_ref, g2_ref,
    own, halo, rows_scr, cot3, act3, src3, gp3, preT, wcat, gp_halo, gin_f, gin_v,
    parts, rx0, rx1, rx2, rx3,
    load_sem, out_sem, hs, hr, gs, gr, send_sem, recv_sem,
):
    nx, nzh, ny, nzl, scale = cfg
    nq = nx * ny
    nz = nzh * nzl
    per = TILES // (2 * nq)
    half = TILES // 2
    nsp = ny * nzl
    dp = lax.axis_index("dp")
    sp = lax.axis_index("space")
    core = lax.rem(dp, 2)
    zh = lax.rem(dp // 2, nzh)
    x = dp // (2 * nzh)
    y = sp // nzl
    zl = lax.rem(sp, nzl)
    q = x * ny + y
    z = zh * nzl + zl
    me = core * nq + q

    def plane_peer(slot):
        c = slot // nq
        r = lax.rem(slot, nq)
        return (((r // ny) * nzh + zh) * 2 + c, lax.rem(r, ny) * nzl + zl)

    def z_peer(other):
        return ((x * nzh + other // nzl) * 2 + core, y * nzl + lax.rem(other, nzl))

    has_prev = sp > 0
    has_next = sp < nsp - 1
    barrier = pltpu.get_barrier_semaphore()

    @pl.when(has_prev)
    def _():
        pl.semaphore_signal(barrier, inc=1, device_id=(dp, sp - 1))

    @pl.when(has_next)
    def _():
        pl.semaphore_signal(barrier, inc=1, device_id=(dp, sp + 1))

    def greet_plane(k, carry):
        pl.semaphore_signal(barrier, inc=1, device_id=plane_peer(lax.rem(me + k, 2 * nq)))
        return carry

    def greet_z(k, carry):
        pl.semaphore_signal(barrier, inc=1, device_id=z_peer(lax.rem(z + k, nz)))
        return carry

    lax.fori_loop(1, 2 * nq, greet_plane, 0)
    lax.fori_loop(1, nz, greet_z, 0)

    args = (cot_hbm, src_hbm, pre_hbm)
    loads = [pltpu.make_async_copy(args[k].at[0], own.at[k], load_sem.at[k]) for k in range(3)]
    for copy in loads:
        copy.start()

    expected = 2 * nq - 1 + nz - 1 + has_prev.astype(jnp.int32) + has_next.astype(jnp.int32)
    pl.semaphore_wait(barrier, expected)

    def halo_copy(k, side):
        return pltpu.make_async_remote_copy(
            src_ref=args[k].at[0, :, side],
            dst_ref=halo.at[k, 1 - side],
            send_sem=hs.at[k, side],
            recv_sem=hr.at[k, 1 - side],
            device_id=(dp, sp - 1 if side == 0 else sp + 1),
        )

    for side, there in ((0, has_prev), (1, has_next)):
        @pl.when(there)
        def _():
            for k in range(3):
                halo_copy(k, side).start()

        @pl.when(jnp.logical_not(there))
        def _():
            halo[:, side] = jnp.zeros((3, CH, HGT, WID), BF16)

    for g, w_ref in ((0, w1_ref), (1, w2_ref)):
        for a in range(3):
            for b in range(3):
                block = w_ref[a, b].reshape(3 * CH, CH).astype(F32)
                wcat[g, b * CH:(b + 1) * CH, (2 - a) * 96:(3 - a) * 96] = block.T.astype(BF16)

    lane = lax.broadcasted_iota(jnp.int32, (CH, WID), 1)

    def shifts(value):
        up = jnp.where(lane < WID - 1, pltpu.roll(value, WID - 1, 1), 0.0)
        down = jnp.where(lane > 0, pltpu.roll(value, 1, 1), 0.0)
        return (up, value, down)

    def put_shifted(ref, p, h, value):
        for c, moved in enumerate(shifts(value)):
            ref[p * 96 + c * CH:p * 96 + (c + 1) * CH, h * WID:(h + 1) * WID] = moved.astype(BF16)

    def put_rows(ref, p, h, value):
        moved = value.astype(BF16)
        for b in range(3):
            to = h - b + 1
            if 0 <= to < HGT:
                ref[p * 96 + b * CH:p * 96 + (b + 1) * CH, to * WID:(to + 1) * WID] = moved

    def clear_edges(ref, p):
        blank = jnp.zeros((CH, WID), BF16)
        ref[p * 96:p * 96 + CH, 0:WID] = blank
        ref[p * 96 + 2 * CH:p * 96 + 3 * CH, (HGT - 1) * WID:HGT * WID] = blank

    def turned(k, p, plane):
        rows_scr[k, p] = plane.astype(F32).reshape(CH * HGT, WID)
        return [rows_scr[k, p, pl.ds(h, CH, stride=HGT), :] for h in range(HGT)]

    def take(k, p, plane):
        for h, value in enumerate(turned(k, p, plane)):
            if k == 0:
                put_shifted(cot3, p, h, value)
            elif k == 1:
                put_rows(src3, p, h, value)
            else:
                put_rows(act3, p, h, leaky(value))
                if 1 <= p <= 2:
                    preT[p - 1, :, h * WID:(h + 1) * WID] = value

    for p in range(4):
        clear_edges(src3, p)
        clear_edges(act3, p)
    for k in range(3):
        loads[k].wait()
        for d in range(2):
            take(k, d + 1, own[k, :, d])

    for k in range(3):
        for side, there in ((0, has_prev), (1, has_next)):
            @pl.when(there)
            def _():
                halo_copy(k, 1 - side).wait_recv()
            take(k, 3 * side, halo[k, side])

    def conv(g, ref, d):
        y3 = jnp.dot(wcat[g], ref[d * 96:(d + 3) * 96, :], preferred_element_type=F32)
        blank = jnp.zeros((CH, WID), F32)
        first = jnp.concatenate([y3[0:CH, WID:], blank], axis=1)
        last = jnp.concatenate([blank, y3[2 * CH:, :PLANE - WID]], axis=1)
        return y3[CH:2 * CH] + first + last

    def kernel_grad(low, top):
        total = None
        for d in range(2):
            term = lax.dot_general(
                low[d * 96:(d + 3) * 96, :],
                top[(d + 1) * 96:(d + 1) * 96 + 128, :],
                (((1,), (1,)), ((), ())),
                preferred_element_type=F32,
            )
            total = term if total is None else total + term
        return total

    lane8 = lax.broadcasted_iota(jnp.int32, (9, 8, 128), 2) // CH

    def pack(g, total):
        rows = total.reshape(9, 4, 8, 128)
        for c in range(3):
            tile = None
            for j in range(4):
                piece = rows[:, j]
                shift = ((j - c) * CH) % 128
                if shift:
                    piece = pltpu.roll(piece, shift, 2)
                tile = piece if tile is None else jnp.where(lane8 == j, piece, tile)
            for ab in range(9):
                parts[g, ab * 3 + c] = tile[ab]
        for t in range(USED, TILES):
            parts[g, t] = jnp.zeros((8, 128), F32)

    def rdma(src, dst, g, phase, device):
        return pltpu.make_async_remote_copy(
            src_ref=src, dst_ref=dst, send_sem=send_sem.at[g, phase], recv_sem=recv_sem.at[g, phase], device_id=device
        )

    def pair(g):
        other = 1 - core
        return rdma(parts.at[g, pl.ds(other * half, half)], rx0.at[g], g, 0, (dp + other - core, sp))

    def phase1(g):
        pair(g).wait_recv()
        rx0[g] = rx0[g] + parts[g, pl.ds(core * half, half)]
        rx1[g, q] = rx0[g, pl.ds(q * per, per)]

        def send(k, carry):
            r = lax.rem(q + k, nq)
            rdma(rx0.at[g, pl.ds(r * per, per)], rx1.at[g, q], g, 1, plane_peer(core * nq + r)).start()
            return carry

        lax.fori_loop(1, nq, send, 0)

    def all_of(ref, g, phase, count):
        return rdma(ref.at[g, pl.ds(0, count)], ref.at[g, pl.ds(0, count)], g, phase, (dp + 1 - 2 * core, sp))

    def phase2(g):
        all_of(rx1, g, 1, nq - 1).wait_recv()
        total = rx1[g, 0]
        for r in range(1, nq):
            total = total + rx1[g, r]
        rx2[g, z] = total

        def send(k, carry):
            rdma(rx2.at[g, z], rx2.at[g, z], g, 2, z_peer(lax.rem(z + k, nz))).start()
            return carry

        lax.fori_loop(1, nz, send, 0)

    def phase3(g):
        all_of(rx2, g, 2, nz - 1).wait_recv()
        total = rx2[g, 0]
        for r in range(1, nz):
            total = total + rx2[g, r]
        total = total * scale
        for t in range(per):
            tile = total[t]
            square = jnp.concatenate(
                [tile] + [pltpu.roll(tile, 128 - CH * j, 1) for j in range(1, 4)] + [jnp.zeros((96, 128), F32)], axis=0
            ).T
            mine = None
            for j in range(4):
                piece = square[8 * j:8 * (j + 1)]
                if j:
                    piece = pltpu.roll(piece, CH * j, 1)
                mine = piece if mine is None else mine + piece
            rx3[g, me, t] = mine

        def send(k, carry):
            rdma(rx3.at[g, me], rx3.at[g, me], g, 3, plane_peer(lax.rem(me + k, 2 * nq))).start()
            return carry

        lax.fori_loop(1, 2 * nq, send, 0)

    def finish(g, out_ref):
        all_of(rx3, g, 3, 2 * nq - 1).wait_recv()
        tiles = rx3[g].reshape(TILES, 8, 128)[:USED]
        for j in range(4):
            piece = tiles if j == 0 else pltpu.roll(tiles, 128 - CH * j, 2)
            out_ref[:, 8 * j:8 * (j + 1), :] = piece[:, :, :CH]

    for d in range(2):
        value = conv(1, cot3, d) * jnp.where(preT[d] > 0, 1.0, 0.3)
        for h in range(HGT):
            put_shifted(gp3, d + 1, h, value[:, h * WID:(h + 1) * WID].astype(BF16).astype(F32))

    def gp_copy(side):
        return pltpu.make_async_remote_copy(
            src_ref=gp3.at[pl.ds((1 + side) * 96 + CH, CH)],
            dst_ref=gp_halo.at[1 - side],
            send_sem=gs.at[side],
            recv_sem=gr.at[1 - side],
            device_id=(dp, sp - 1 if side == 0 else sp + 1),
        )

    for side, there in ((0, has_prev), (1, has_next)):
        @pl.when(there)
        def _():
            gp_copy(side).start()

        @pl.when(jnp.logical_not(there))
        def _():
            gp_halo[side] = jnp.zeros((CH, PLANE), BF16)

    gp3[0:96, :] = jnp.zeros((96, PLANE), BF16)
    gp3[288:384, :] = jnp.zeros((96, PLANE), BF16)
    pack(0, kernel_grad(src3, gp3))
    pair(0).start()
    pack(1, kernel_grad(act3, cot3))
    pair(1).start()
    phase1(0)
    phase1(1)

    for side, there in ((0, has_prev), (1, has_next)):
        @pl.when(there)
        def _():
            gp_copy(1 - side).wait_recv()
        for h in range(HGT):
            put_shifted(gp3, 3 * side, h, gp_halo[side, :, h * WID:(h + 1) * WID].astype(F32))
    phase2(0)
    phase2(1)
    for d in range(2):
        value = conv(0, gp3, d)
        for h in range(HGT):
            gin_f[d, pl.ds(h, CH, stride=HGT), :] = value[:, h * WID:(h + 1) * WID]
        gin_v[:, d] = gin_f[d].reshape(CH, HGT, WID).astype(BF16)
    out_copy = pltpu.make_async_copy(gin_v, gin_hbm.at[0], out_sem)
    out_copy.start()
    phase3(0)
    phase3(1)
    finish(0, g1_ref)
    finish(1, g2_ref)
    out_copy.wait()

    for side, there in ((0, has_prev), (1, has_next)):
        @pl.when(there)
        def _():
            for k in range(3):
                halo_copy(k, side).wait_send()
            gp_copy(side).wait_send()
    for g in range(2):
        pair(g).wait_send()
        all_of(rx1, g, 1, nq - 1).wait_send()
        all_of(rx2, g, 2, nz - 1).wait_send()
        all_of(rx3, g, 3, 2 * nq - 1).wait_send()


def build(mesh, sizes):
    nx, nzh, ny, nzl = sizes
    nq = nx * ny
    nz = nzh * nzl
    per = TILES // (2 * nq)
    total = mesh.shape["dp"] * mesh.shape["space"] * 2 * HGT * WID
    cfg = (nx, nzh, ny, nzl, float(total) ** -0.5)
    any_spec = pl.BlockSpec(memory_space=pl.ANY)
    vmem = pl.BlockSpec(memory_space=pltpu.VMEM)
    dma = pltpu.SemaphoreType.DMA

    def per_device(layer_input, pre_act, cotangent, weight_one, weight_two):
        gin, g1, g2 = pl.pallas_call(
            functools.partial(kernel, cfg),
            out_shape=(
                jax.ShapeDtypeStruct(layer_input.shape, BF16),
                jax.ShapeDtypeStruct((USED, CH, CH), F32),
                jax.ShapeDtypeStruct((USED, CH, CH), F32),
            ),
            in_specs=[any_spec, any_spec, any_spec, vmem, vmem],
            out_specs=(any_spec, vmem, vmem),
            scratch_shapes=[
                pltpu.VMEM((3, CH, 2, HGT, WID), BF16),
                pltpu.VMEM((3, 2, CH, HGT, WID), BF16),
                pltpu.VMEM((3, 4, CH * HGT, WID), F32),
                pltpu.VMEM((384, PLANE), BF16),
                pltpu.VMEM((384, PLANE), BF16),
                pltpu.VMEM((384, PLANE), BF16),
                pltpu.VMEM((384, PLANE), BF16),
                pltpu.VMEM((2, CH, PLANE), F32),
                pltpu.VMEM((2, 96, 288), BF16),
                pltpu.VMEM((2, CH, PLANE), BF16),
                pltpu.VMEM((2, CH * HGT, WID), F32),
                pltpu.VMEM((CH, 2, HGT, WID), BF16),
                pltpu.VMEM((2, TILES, 8, 128), F32),
                pltpu.VMEM((2, TILES // 2, 8, 128), F32),
                pltpu.VMEM((2, nq, per, 8, 128), F32),
                pltpu.VMEM((2, nz, per, 8, 128), F32),
                pltpu.VMEM((2, 2 * nq, per, 8, 128), F32),
                dma((3,)),
                dma,
                dma((3, 2)),
                dma((3, 2)),
                dma((2,)),
                dma((2,)),
                dma((2, 4)),
                dma((2, 4)),
            ],
            compiler_params=pltpu.CompilerParams(
                collective_id=0, has_side_effects=True, vmem_limit_bytes=48 * 1024 * 1024
            ),
        )(layer_input, pre_act, cotangent, weight_one, weight_two)
        shape = weight_one.shape
        return gin, g1.reshape(shape), g2.reshape(shape)

    split = P("dp", None, "space", None, None)
    return jax.shard_map(
        per_device,
        mesh=mesh,
        in_specs=(split, split, split, P(), P()),
        out_specs=(split, P(), P()),
        check_vma=False,
    )


def solution(mesh):
    nzl = 2
    ny = mesh.shape["space"] // nzl
    nx = 4
    nzh = mesh.shape["dp"] // (2 * nx)
    return build(mesh, (nx, nzh, ny, nzl))
```

```python
import functools

import jax
import jax.numpy as jnp
from jax import lax
from jax.experimental import pallas as pl
from jax.experimental.pallas import tpu as pltpu
from jax.sharding import PartitionSpec as P

CH = 32
HGT = 16
WID = 128
PLANE = HGT * WID
TILES = 32
USED = 27
F32 = jnp.float32
BF16 = jnp.bfloat16


def leaky(value):
    return jnp.where(value > 0, value, 0.3 * value)


def kernel(
    cfg,
    src_hbm, pre_hbm, cot_hbm, w1_hbm, w2_hbm,
    gin_ref, g1_ref, g2_ref,
    own, weights, halo, rows_scr, cot3, act3, src3, gp3, preT, wcat, gp_halo, gin_f, gacc,
    parts, rx0, rx1, rx2, rx3,
    load_sem, known_x, known_y, known_z, known_c, hs, hr, gs, gr, send_sem, recv_sem,
):
    nx, nzh, ny, nzl, scale = cfg
    nq = nx * ny
    nz = nzh * nzl
    per = TILES // (2 * nq)
    half = TILES // 2
    nsp = ny * nzl
    dp = lax.axis_index("dp")
    sp = lax.axis_index("space")
    core = lax.rem(dp, 2)
    zh = lax.rem(dp // 2, nzh)
    x = dp // (2 * nzh)
    y = sp // nzl
    zl = lax.rem(sp, nzl)
    q = x * ny + y
    z = zh * nzl + zl
    me = core * nq + q

    def plane_peer(slot):
        c = slot // nq
        r = lax.rem(slot, nq)
        return (((r // ny) * nzh + zh) * 2 + c, lax.rem(r, ny) * nzl + zl)

    def z_peer(other):
        return ((x * nzh + other // nzl) * 2 + core, y * nzl + lax.rem(other, nzl))

    has_prev = sp > 0
    has_next = sp < nsp - 1
    barrier = pltpu.get_barrier_semaphore()
    partner = (dp + 1 - 2 * core, sp)

    def at_x(r):
        return ((r * nzh + zh) * 2 + core, sp)

    def at_y(r):
        return (dp, r * nzl + zl)

    beside_x = (at_x(lax.rem(x + 1, nx)), at_x(lax.rem(x + nx - 1, nx)))
    beside_y = (at_y(lax.rem(y + 1, ny)), at_y(lax.rem(y + ny - 1, ny)))
    beside_z = (z_peer(lax.rem(z + 1, nz)), z_peer(lax.rem(z + nz - 1, nz)))

    @pl.when(has_prev)
    def _():
        pl.semaphore_signal(barrier, inc=1, device_id=(dp, sp - 1))

    @pl.when(has_next)
    def _():
        pl.semaphore_signal(barrier, inc=1, device_id=(dp, sp + 1))

    for device in beside_x + beside_y + beside_z + (partner,):
        pl.semaphore_signal(barrier, inc=1, device_id=device)

    args = (cot_hbm, src_hbm, pre_hbm)
    loads = [pltpu.make_async_copy(args[k].at[0], own.at[k], load_sem.at[k]) for k in (0, 1, 2)]
    weight_loads = [
        pltpu.make_async_copy((w1_hbm, w2_hbm)[g], weights.at[g], load_sem.at[3 + g]) for g in range(2)
    ]
    for copy in (loads[0], weight_loads[1], loads[2], loads[1], weight_loads[0]):
        copy.start()

    pl.semaphore_wait(barrier, 7 + has_prev.astype(jnp.int32) + has_next.astype(jnp.int32))

    def halo_copy(k, side):
        return pltpu.make_async_remote_copy(
            src_ref=args[k].at[0, :, side],
            dst_ref=halo.at[k, 1 - side],
            send_sem=hs.at[k, side],
            recv_sem=hr.at[k, 1 - side],
            device_id=(dp, sp - 1 if side == 0 else sp + 1),
        )

    sides = ((0, has_prev), (1, has_next))
    for k in range(2):
        for side, there in sides:
            @pl.when(there)
            def _():
                halo_copy(k, side).start()

    for side, there in sides:
        @pl.when(jnp.logical_not(there))
        def _():
            halo[:, side] = jnp.zeros((2, CH, HGT, WID), BF16)

    def tell(sem, step, devices):
        for device in devices:
            pl.semaphore_signal(sem.at[step], inc=1, device_id=device)

    def learn(sem, step, count=2):
        pl.semaphore_wait(sem.at[step], count)

    tell(known_x, 0, beside_x)
    tell(known_z, 0, beside_z)

    def spread(g):
        weight_loads[g].wait()
        for a in range(3):
            for b in range(3):
                block = weights[g, a, b].reshape(3 * CH, CH).astype(F32)
                wcat[g, b * CH:(b + 1) * CH, (2 - a) * 96:(3 - a) * 96] = block.T.astype(BF16)

    spread(1)

    lane = lax.broadcasted_iota(jnp.int32, (CH, WID), 1)

    def shifts(value):
        up = jnp.where(lane < WID - 1, pltpu.roll(value, WID - 1, 1), 0.0)
        down = jnp.where(lane > 0, pltpu.roll(value, 1, 1), 0.0)
        return (up, value, down)

    def put_shifted(ref, p, h, value):
        for c, moved in enumerate(shifts(value)):
            ref[p * 96 + c * CH:p * 96 + (c + 1) * CH, h * WID:(h + 1) * WID] = moved.astype(BF16)

    def put_rows(ref, p, h, value):
        moved = value.astype(BF16)
        for b in range(3):
            to = h - b + 1
            if 0 <= to < HGT:
                ref[p * 96 + b * CH:p * 96 + (b + 1) * CH, to * WID:(to + 1) * WID] = moved

    def clear_edges(ref, p):
        blank = jnp.zeros((CH, WID), BF16)
        ref[p * 96:p * 96 + CH, 0:WID] = blank
        ref[p * 96 + 2 * CH:p * 96 + 3 * CH, (HGT - 1) * WID:HGT * WID] = blank

    def turned(k, p, plane):
        rows_scr[k, p] = plane.astype(F32).reshape(CH * HGT, WID)
        return [rows_scr[k, p, pl.ds(h, CH, stride=HGT), :] for h in range(HGT)]

    def take(k, p, plane):
        for h, value in enumerate(turned(k, p, plane)):
            if k == 0:
                put_shifted(cot3, p, h, value)
            elif k == 1:
                put_rows(src3, p, h, value)
            else:
                put_rows(act3, p - 1, h, leaky(value))
                preT[p - 1, :, h * WID:(h + 1) * WID] = value

    def conv(g, ref, d):
        y3 = jnp.dot(wcat[g], ref[d * 96:(d + 3) * 96, :], preferred_element_type=F32)
        blank = jnp.zeros((CH, WID), F32)
        first = jnp.concatenate([y3[0:CH, WID:], blank], axis=1)
        last = jnp.concatenate([blank, y3[2 * CH:, :PLANE - WID]], axis=1)
        return y3[CH:2 * CH] + first + last

    def kernel_grad(low, top):
        total = None
        for d in range(2):
            term = lax.dot_general(
                low[d * 96:(d + 3) * 96, :],
                top[(d + 1) * 96:(d + 1) * 96 + 128, :],
                (((1,), (1,)), ((), ())),
                preferred_element_type=F32,
            )
            total = term if total is None else total + term
        return total

    def partial(low, top):
        return lax.dot_general(low, top, (((1,), (1,)), ((), ())), preferred_element_type=F32)

    lane8 = lax.broadcasted_iota(jnp.int32, (9, 8, 128), 2) // CH

    def pack(g, total):
        rows = total.reshape(9, 4, 8, 128)
        for c in range(3):
            tile = None
            for j in range(4):
                piece = rows[:, j]
                shift = ((j - c) * CH) % 128
                if shift:
                    piece = pltpu.roll(piece, shift, 2)
                tile = piece if tile is None else jnp.where(lane8 == j, piece, tile)
            for ab in range(9):
                parts[g, ab * 3 + c] = tile[ab]
        for t in range(USED, TILES):
            parts[g, t] = jnp.zeros((8, 128), F32)

    def rdma(src, dst, g, phase, device):
        return pltpu.make_async_remote_copy(
            src_ref=src, dst_ref=dst, send_sem=send_sem.at[g, phase], recv_sem=recv_sem.at[g, phase], device_id=device
        )

    def pair(g):
        other = 1 - core
        return rdma(parts.at[g, pl.ds(other * half, half)], rx0.at[g], g, 0, partner)

    def phase1(g):
        pair(g).wait_recv()
        rx0[g] = rx0[g] + parts[g, pl.ds(core * half, half)]
        rx1[g, q] = rx0[g, pl.ds(q * per, per)]

        def send(k, carry):
            r = lax.rem(q + k, nq)
            rdma(rx0.at[g, pl.ds(r * per, per)], rx1.at[g, q], g, 1, plane_peer(core * nq + r)).start()
            return carry

        lax.fori_loop(1, nq, send, 0)

    def all_of(ref, g, phase, count):
        return rdma(ref.at[g, pl.ds(0, count)], ref.at[g, pl.ds(0, count)], g, phase, partner)

    def phase2(g):
        all_of(rx1, g, 1, nq - 1).wait_recv()
        total = rx1[g, 0]
        for r in range(1, nq):
            total = total + rx1[g, r]
        rx2[g, z] = total

        def send(k, carry):
            rdma(rx2.at[g, z], rx2.at[g, z], g, 2, z_peer(lax.rem(z + k, nz))).start()
            return carry

        lax.fori_loop(1, nz, send, 0)

    def phase3(g):
        all_of(rx2, g, 2, nz - 1).wait_recv()
        total = rx2[g, 0]
        for r in range(1, nz):
            total = total + rx2[g, r]
        total = total * scale
        for t in range(per):
            tile = total[t]
            square = jnp.concatenate(
                [tile] + [pltpu.roll(tile, 128 - CH * j, 1) for j in range(1, 4)] + [jnp.zeros((96, 128), F32)], axis=0
            ).T
            mine = None
            for j in range(4):
                piece = square[8 * j:8 * (j + 1)]
                if j:
                    piece = pltpu.roll(piece, CH * j, 1)
                mine = piece if mine is None else mine + piece
            rx3[g, me, t] = mine

        def send(k, carry):
            rdma(rx3.at[g, me], rx3.at[g, me], g, 3, plane_peer(lax.rem(me + k, 2 * nq))).start()
            return carry

        lax.fori_loop(1, 2 * nq, send, 0)

    def finish(g, out_ref):
        all_of(rx3, g, 3, 2 * nq - 1).wait_recv()
        tiles = rx3[g].reshape(TILES, 8, 128)[:USED]
        for j in range(4):
            piece = tiles if j == 0 else pltpu.roll(tiles, 128 - CH * j, 2)
            out_ref[:, 8 * j:8 * (j + 1), :] = piece[:, :, :CH]

    def gp_copy(side):
        return pltpu.make_async_remote_copy(
            src_ref=gp3.at[pl.ds((1 + side) * 96 + CH, CH)],
            dst_ref=gp_halo.at[1 - side],
            send_sem=gs.at[side],
            recv_sem=gr.at[1 - side],
            device_id=(dp, sp - 1 if side == 0 else sp + 1),
        )

    loads[0].wait()
    for d in range(2):
        take(0, d + 1, own[0, :, d])
    learn(known_x, 0)
    learn(known_z, 0)
    tell(known_y, 0, beside_y)
    tell(known_z, 1, beside_z)
    for p in range(2):
        clear_edges(act3, p)
    loads[2].wait()
    for d in range(2):
        take(2, d + 1, own[2, :, d])
    learn(known_y, 0)
    learn(known_z, 1)
    tell(known_y, 1, beside_y)
    tell(known_z, 2, beside_z)
    for p in range(4):
        clear_edges(src3, p)
    loads[1].wait()
    for d in range(2):
        take(1, d + 1, own[1, :, d])
    learn(known_y, 1)
    learn(known_z, 2)
    tell(known_c, 0, (partner,))
    here = partial(act3[...], cot3[96:224, :])
    gacc[96:288] = here
    here = partial(act3[...], cot3[192:320, :])
    gacc[0:96] = here[:96]
    gacc[96:192] += here[96:]
    spread(0)

    for side, there in sides:
        @pl.when(there)
        def _():
            halo_copy(0, 1 - side).wait_recv()
        take(0, 3 * side, halo[0, side])
        value = conv(1, cot3, side) * jnp.where(preT[side] > 0, 1.0, 0.3)
        for h in range(HGT):
            put_shifted(gp3, side + 1, h, value[:, h * WID:(h + 1) * WID].astype(BF16).astype(F32))

        @pl.when(there)
        def _():
            gp_copy(side).start()

        @pl.when(jnp.logical_not(there))
        def _():
            gp_halo[side] = jnp.zeros((CH, PLANE), BF16)

    for side, there in sides:
        @pl.when(there)
        def _():
            halo_copy(1, 1 - side).wait_recv()
        take(1, 3 * side, halo[1, side])
    pack(0, kernel_grad(src3, gp3))
    pair(0).start()
    gacc[192:288] += partial(act3[0:96, :], cot3[0:128, :])
    gacc[0:96] += partial(act3[96:192, :], cot3[288:416, :])
    pack(1, gacc[...])
    pair(1).start()
    phase1(0)
    phase1(1)
    learn(known_c, 0, 1)
    phase2(0)
    phase2(1)
    for side, there in sides:
        @pl.when(there)
        def _():
            gp_copy(1 - side).wait_recv()
        for h in range(HGT):
            put_shifted(gp3, 3 * side, h, gp_halo[side, :, h * WID:(h + 1) * WID].astype(F32))
    for d in range(2):
        value = conv(0, gp3, d)
        for h in range(HGT):
            gin_f[d, pl.ds(h, CH, stride=HGT), :] = value[:, h * WID:(h + 1) * WID]
        gin_ref[0, :, d] = gin_f[d].reshape(CH, HGT, WID).astype(BF16)
    phase3(0)
    phase3(1)
    finish(0, g1_ref)
    finish(1, g2_ref)

    for side, there in sides:
        @pl.when(there)
        def _():
            for k in range(2):
                halo_copy(k, side).wait_send()
            gp_copy(side).wait_send()
    for g in range(2):
        pair(g).wait_send()
        all_of(rx1, g, 1, nq - 1).wait_send()
        all_of(rx2, g, 2, nz - 1).wait_send()
        all_of(rx3, g, 3, 2 * nq - 1).wait_send()


def write_out(gin_ref, g1_ref, g2_ref, gin_hbm, g1_hbm, g2_hbm, sem):
    pairs = ((gin_ref, gin_hbm), (g1_ref, g1_hbm), (g2_ref, g2_hbm))
    copies = [pltpu.make_async_copy(here, there, sem.at[k]) for k, (here, there) in enumerate(pairs)]
    for copy in copies:
        copy.start()
    for copy in copies:
        copy.wait()


def build(mesh, sizes):
    nx, nzh, ny, nzl = sizes
    nq = nx * ny
    nz = nzh * nzl
    per = TILES // (2 * nq)
    total = mesh.shape["dp"] * mesh.shape["space"] * 2 * HGT * WID
    cfg = (nx, nzh, ny, nzl, float(total) ** -0.5)
    hbm = pl.BlockSpec(memory_space=pltpu.HBM)
    vmem = pl.BlockSpec(memory_space=pltpu.VMEM)
    dma = pltpu.SemaphoreType.DMA

    def per_device(layer_input, pre_act, cotangent, weight_one, weight_two):
        held = [
            pltpu.with_memory_space_constraint(v, pltpu.HBM)
            for v in (layer_input, pre_act, cotangent, weight_one, weight_two)
        ]
        gin, g1, g2 = pl.pallas_call(
            functools.partial(kernel, cfg),
            out_shape=(
                jax.ShapeDtypeStruct(layer_input.shape, BF16),
                jax.ShapeDtypeStruct((USED, CH, CH), F32),
                jax.ShapeDtypeStruct((USED, CH, CH), F32),
            ),
            in_specs=[hbm] * 5,
            out_specs=(vmem, vmem, vmem),
            scratch_shapes=[
                pltpu.VMEM((3, CH, 2, HGT, WID), BF16),
                pltpu.VMEM((2, 3, 3, 3, CH, CH), BF16),
                pltpu.VMEM((2, 2, CH, HGT, WID), BF16),
                pltpu.VMEM((3, 4, CH * HGT, WID), F32),
                pltpu.VMEM((416, PLANE), BF16),
                pltpu.VMEM((192, PLANE), BF16),
                pltpu.VMEM((384, PLANE), BF16),
                pltpu.VMEM((384, PLANE), BF16),
                pltpu.VMEM((2, CH, PLANE), F32),
                pltpu.VMEM((2, 96, 288), BF16),
                pltpu.VMEM((2, CH, PLANE), BF16),
                pltpu.VMEM((2, CH * HGT, WID), F32),
                pltpu.VMEM((288, 128), F32),
                pltpu.VMEM((2, TILES, 8, 128), F32),
                pltpu.VMEM((2, TILES // 2, 8, 128), F32),
                pltpu.VMEM((2, nq, per, 8, 128), F32),
                pltpu.VMEM((2, nz, per, 8, 128), F32),
                pltpu.VMEM((2, 2 * nq, per, 8, 128), F32),
                dma((5,)),
                pltpu.SemaphoreType.REGULAR((1,)),
                pltpu.SemaphoreType.REGULAR((2,)),
                pltpu.SemaphoreType.REGULAR((3,)),
                pltpu.SemaphoreType.REGULAR((1,)),
                dma((2, 2)),
                dma((2, 2)),
                dma((2,)),
                dma((2,)),
                dma((2, 4)),
                dma((2, 4)),
            ],
            compiler_params=pltpu.CompilerParams(
                collective_id=0, has_side_effects=True, vmem_limit_bytes=48 * 1024 * 1024
            ),
        )(*held)
        gin, g1, g2 = pl.pallas_call(
            write_out,
            out_shape=tuple(jax.ShapeDtypeStruct(v.shape, v.dtype) for v in (gin, g1, g2)),
            in_specs=[vmem] * 3,
            out_specs=(hbm,) * 3,
            scratch_shapes=[dma((3,))],
            compiler_params=pltpu.CompilerParams(vmem_limit_bytes=8 * 1024 * 1024),
        )(gin, g1, g2)
        shape = weight_one.shape
        return gin, g1.reshape(shape), g2.reshape(shape)

    split = P("dp", None, "space", None, None)
    return jax.shard_map(
        per_device,
        mesh=mesh,
        in_specs=(split, split, split, P(), P()),
        out_specs=(split, P(), P()),
        check_vma=False,
    )


def solution(mesh):
    nzl = 2
    ny = mesh.shape["space"] // nzl
    nx = 4
    nzh = mesh.shape["dp"] // (2 * nx)
    return build(mesh, (nx, nzh, ny, nzl))
```

```python
import functools

import jax
import jax.numpy as jnp
from jax import lax
from jax.experimental import pallas as pl
from jax.experimental.pallas import tpu as pltpu
from jax.sharding import PartitionSpec as P

CH = 32
HGT = 16
WID = 128
PLANE = HGT * WID
TILES = 32
USED = 27
F32 = jnp.float32
BF16 = jnp.bfloat16


def leaky(value):
    return jnp.where(value > 0, value, 0.3 * value)


def kernel(
    cfg,
    src_hbm, pre_hbm, cot_hbm, w1_hbm, w2_hbm,
    gin_ref, g1_ref, g2_ref,
    own, weights, halo, rows_scr, cot3, act3, src3, gp3, preT, wcat, gp_halo, gin_f, gacc,
    parts, rx0, rx1, rx2, rx3,
    load_sem, known_x, known_y, known_z, known_c, hs, hr, gs, gr, send_sem, recv_sem,
):
    nx, nzh, ny, nzl, scale = cfg
    nq = nx * ny
    nz = nzh * nzl
    per = TILES // (2 * nq)
    half = TILES // 2
    nsp = ny * nzl
    dp = lax.axis_index("dp")
    sp = lax.axis_index("space")
    core = lax.rem(dp, 2)
    zh = lax.rem(dp // 2, nzh)
    x = dp // (2 * nzh)
    y = sp // nzl
    zl = lax.rem(sp, nzl)
    q = x * ny + y
    z = zh * nzl + zl
    me = core * nq + q

    def plane_peer(slot):
        c = slot // nq
        r = lax.rem(slot, nq)
        return (((r // ny) * nzh + zh) * 2 + c, lax.rem(r, ny) * nzl + zl)

    def z_peer(other):
        return ((x * nzh + other // nzl) * 2 + core, y * nzl + lax.rem(other, nzl))

    has_prev = sp > 0
    has_next = sp < nsp - 1
    barrier = pltpu.get_barrier_semaphore()
    partner = (dp + 1 - 2 * core, sp)

    def at_x(r):
        return ((r * nzh + zh) * 2 + core, sp)

    def at_y(r):
        return (dp, r * nzl + zl)

    beside_x = (at_x(lax.rem(x + 1, nx)), at_x(lax.rem(x + nx - 1, nx)))
    beside_y = (at_y(lax.rem(y + 1, ny)), at_y(lax.rem(y + ny - 1, ny)))
    beside_z = (z_peer(lax.rem(z + 1, nz)), z_peer(lax.rem(z + nz - 1, nz)))

    @pl.when(has_prev)
    def _():
        pl.semaphore_signal(barrier, inc=1, device_id=(dp, sp - 1))

    @pl.when(has_next)
    def _():
        pl.semaphore_signal(barrier, inc=1, device_id=(dp, sp + 1))

    for device in beside_x + beside_y + beside_z + (partner,):
        pl.semaphore_signal(barrier, inc=1, device_id=device)

    args = (cot_hbm, src_hbm, pre_hbm)
    loads = [pltpu.make_async_copy(args[k].at[0], own.at[k], load_sem.at[k]) for k in (0, 1, 2)]
    weight_loads = [
        pltpu.make_async_copy((w1_hbm, w2_hbm)[g], weights.at[g], load_sem.at[3 + g]) for g in range(2)
    ]
    for copy in (loads[0], weight_loads[1], loads[2], loads[1], weight_loads[0]):
        copy.start()

    pl.semaphore_wait(barrier, 7 + has_prev.astype(jnp.int32) + has_next.astype(jnp.int32))

    def halo_copy(k, side):
        return pltpu.make_async_remote_copy(
            src_ref=args[k].at[0, :, side],
            dst_ref=halo.at[k, 1 - side],
            send_sem=hs.at[k, side],
            recv_sem=hr.at[k, 1 - side],
            device_id=(dp, sp - 1 if side == 0 else sp + 1),
        )

    sides = ((0, has_prev), (1, has_next))
    for k in range(2):
        for side, there in sides:
            @pl.when(there)
            def _():
                halo_copy(k, side).start()

    for side, there in sides:
        @pl.when(jnp.logical_not(there))
        def _():
            halo[:, side] = jnp.zeros((2, CH, HGT, WID), BF16)

    def tell(sem, step, devices):
        for device in devices:
            pl.semaphore_signal(sem.at[step], inc=1, device_id=device)

    def learn(sem, step, count=2):
        pl.semaphore_wait(sem.at[step], count)

    tell(known_x, 0, beside_x)
    tell(known_z, 0, beside_z)

    def spread(g):
        weight_loads[g].wait()
        for a in range(3):
            for b in range(3):
                block = weights[g, a, b].reshape(3 * CH, CH).astype(F32)
                wcat[g, b * CH:(b + 1) * CH, (2 - a) * 96:(3 - a) * 96] = block.T.astype(BF16)

    spread(1)

    lane = lax.broadcasted_iota(jnp.int32, (CH, WID), 1)

    def shifts(value):
        up = jnp.where(lane < WID - 1, pltpu.roll(value, WID - 1, 1), 0.0)
        down = jnp.where(lane > 0, pltpu.roll(value, 1, 1), 0.0)
        return (up, value, down)

    def put_shifted(ref, p, h, value):
        for c, moved in enumerate(shifts(value)):
            ref[p * 96 + c * CH:p * 96 + (c + 1) * CH, h * WID:(h + 1) * WID] = moved.astype(BF16)

    def put_rows(ref, p, h, value):
        moved = value.astype(BF16)
        for b in range(3):
            to = h - b + 1
            if 0 <= to < HGT:
                ref[p * 96 + b * CH:p * 96 + (b + 1) * CH, to * WID:(to + 1) * WID] = moved

    def clear_edges(ref, p):
        blank = jnp.zeros((CH, WID), BF16)
        ref[p * 96:p * 96 + CH, 0:WID] = blank
        ref[p * 96 + 2 * CH:p * 96 + 3 * CH, (HGT - 1) * WID:HGT * WID] = blank

    def turned(k, p, plane):
        rows_scr[k, p] = plane.astype(F32).reshape(CH * HGT, WID)
        return [rows_scr[k, p, pl.ds(h, CH, stride=HGT), :] for h in range(HGT)]

    def take(k, p, plane):
        for h, value in enumerate(turned(k, p, plane)):
            if k == 0:
                put_shifted(cot3, p, h, value)
            elif k == 1:
                put_rows(src3, p, h, value)
            else:
                put_rows(act3, p - 1, h, leaky(value))
                preT[p - 1, :, h * WID:(h + 1) * WID] = value

    def conv(g, ref, d):
        y3 = jnp.dot(wcat[g], ref[d * 96:(d + 3) * 96, :], preferred_element_type=F32)
        blank = jnp.zeros((CH, WID), F32)
        first = jnp.concatenate([y3[0:CH, WID:], blank], axis=1)
        last = jnp.concatenate([blank, y3[2 * CH:, :PLANE - WID]], axis=1)
        return y3[CH:2 * CH] + first + last

    def partial(low, top):
        return lax.dot_general(low, top, (((1,), (1,)), ((), ())), preferred_element_type=F32)

    lane8 = lax.broadcasted_iota(jnp.int32, (9, 8, 128), 2) // CH

    def pack(g, total):
        rows = total.reshape(9, 4, 8, 128)
        for c in range(3):
            tile = None
            for j in range(4):
                piece = rows[:, j]
                shift = ((j - c) * CH) % 128
                if shift:
                    piece = pltpu.roll(piece, shift, 2)
                tile = piece if tile is None else jnp.where(lane8 == j, piece, tile)
            for ab in range(9):
                parts[g, ab * 3 + c] = tile[ab]
        for t in range(USED, TILES):
            parts[g, t] = jnp.zeros((8, 128), F32)

    def rdma(src, dst, g, phase, device):
        return pltpu.make_async_remote_copy(
            src_ref=src, dst_ref=dst, send_sem=send_sem.at[g, phase], recv_sem=recv_sem.at[g, phase], device_id=device
        )

    def pair(g):
        other = 1 - core
        return rdma(parts.at[g, pl.ds(other * half, half)], rx0.at[g], g, 0, partner)

    def phase1(g):
        pair(g).wait_recv()
        rx0[g] = rx0[g] + parts[g, pl.ds(core * half, half)]
        rx1[g, q] = rx0[g, pl.ds(q * per, per)]

        def send(k, carry):
            r = lax.rem(q + k, nq)
            rdma(rx0.at[g, pl.ds(r * per, per)], rx1.at[g, q], g, 1, plane_peer(core * nq + r)).start()
            return carry

        lax.fori_loop(1, nq, send, 0)

    def all_of(ref, g, phase, count):
        return rdma(ref.at[g, pl.ds(0, count)], ref.at[g, pl.ds(0, count)], g, phase, partner)

    def phase2(g):
        all_of(rx1, g, 1, nq - 1).wait_recv()
        total = rx1[g, 0]
        for r in range(1, nq):
            total = total + rx1[g, r]
        rx2[g, z] = total

        def send(k, carry):
            rdma(rx2.at[g, z], rx2.at[g, z], g, 2, z_peer(lax.rem(z + k, nz))).start()
            return carry

        lax.fori_loop(1, nz, send, 0)

    def phase3(g):
        all_of(rx2, g, 2, nz - 1).wait_recv()
        total = rx2[g, 0]
        for r in range(1, nz):
            total = total + rx2[g, r]
        total = total * scale
        for t in range(per):
            tile = total[t]
            square = jnp.concatenate(
                [tile] + [pltpu.roll(tile, 128 - CH * j, 1) for j in range(1, 4)] + [jnp.zeros((96, 128), F32)], axis=0
            ).T
            mine = None
            for j in range(4):
                piece = square[8 * j:8 * (j + 1)]
                if j:
                    piece = pltpu.roll(piece, CH * j, 1)
                mine = piece if mine is None else mine + piece
            rx3[g, me, t] = mine

        def send(k, carry):
            rdma(rx3.at[g, me], rx3.at[g, me], g, 3, plane_peer(lax.rem(me + k, 2 * nq))).start()
            return carry

        lax.fori_loop(1, 2 * nq, send, 0)

    def finish(g, out_ref):
        all_of(rx3, g, 3, 2 * nq - 1).wait_recv()
        tiles = rx3[g].reshape(TILES, 8, 128)[:USED]
        for j in range(4):
            piece = tiles if j == 0 else pltpu.roll(tiles, 128 - CH * j, 2)
            out_ref[:, 8 * j:8 * (j + 1), :] = piece[:, :, :CH]

    def gp_copy(side):
        return pltpu.make_async_remote_copy(
            src_ref=gp3.at[pl.ds((1 + side) * 96 + CH, CH)],
            dst_ref=gp_halo.at[1 - side],
            send_sem=gs.at[side],
            recv_sem=gr.at[1 - side],
            device_id=(dp, sp - 1 if side == 0 else sp + 1),
        )

    loads[0].wait()
    for d in range(2):
        take(0, d + 1, own[0, :, d])
    learn(known_x, 0)
    learn(known_z, 0)
    tell(known_y, 0, beside_y)
    tell(known_z, 1, beside_z)
    for p in range(2):
        clear_edges(act3, p)
    loads[2].wait()
    for d in range(2):
        take(2, d + 1, own[2, :, d])
    learn(known_y, 0)
    learn(known_z, 1)
    tell(known_y, 1, beside_y)
    tell(known_z, 2, beside_z)
    for p in range(4):
        clear_edges(src3, p)
    loads[1].wait()
    for d in range(2):
        take(1, d + 1, own[1, :, d])
    learn(known_y, 1)
    learn(known_z, 2)
    tell(known_c, 0, (partner,))
    here = partial(act3[...], cot3[96:224, :])
    gacc[1, 96:288] = here
    here = partial(act3[...], cot3[192:320, :])
    gacc[1, 0:96] = here[:96]
    gacc[1, 96:192] += here[96:]
    spread(0)

    for side, there in sides:
        @pl.when(there)
        def _():
            halo_copy(0, 1 - side).wait_recv()
        take(0, 3 * side, halo[0, side])
        value = conv(1, cot3, side) * jnp.where(preT[side] > 0, 1.0, 0.3)
        for h in range(HGT):
            put_shifted(gp3, side + 1, h, value[:, h * WID:(h + 1) * WID].astype(BF16).astype(F32))

    for side, there in sides:
        @pl.when(there)
        def _():
            gp_copy(side).start()

        @pl.when(jnp.logical_not(there))
        def _():
            gp_halo[side] = jnp.zeros((CH, PLANE), BF16)

    gacc[1, 192:288] += partial(act3[0:96, :], cot3[0:128, :])
    gacc[1, 0:96] += partial(act3[96:192, :], cot3[288:416, :])
    pack(1, gacc[1])
    pair(1).start()
    here = partial(src3[96:288, :], gp3[96:224, :])
    gacc[0, 96:288] = here
    here = partial(src3[96:288, :], gp3[192:320, :])
    gacc[0, 0:96] = here[:96]
    gacc[0, 96:192] += here[96:]
    phase1(1)

    for side, there in sides:
        @pl.when(there)
        def _():
            halo_copy(1, 1 - side).wait_recv()
        take(1, 3 * side, halo[1, side])
        gacc[0, 192 * side:192 * side + 96] += partial(
            src3[288 * side:288 * side + 96, :], gp3[96 * side + 96:96 * side + 224, :]
        )
    pack(0, gacc[0])
    pair(0).start()
    phase1(0)
    phase2(1)
    phase2(0)
    learn(known_c, 0, 1)
    phase3(1)
    for side, there in sides:
        @pl.when(there)
        def _():
            gp_copy(1 - side).wait_recv()
        for h in range(HGT):
            put_shifted(gp3, 3 * side, h, gp_halo[side, :, h * WID:(h + 1) * WID].astype(F32))
    for d in range(2):
        value = conv(0, gp3, d)
        for h in range(HGT):
            gin_f[d, pl.ds(h, CH, stride=HGT), :] = value[:, h * WID:(h + 1) * WID]
        gin_ref[0, :, d] = gin_f[d].reshape(CH, HGT, WID).astype(BF16)
    phase3(0)
    finish(1, g2_ref)
    finish(0, g1_ref)

    for side, there in sides:
        @pl.when(there)
        def _():
            for k in range(2):
                halo_copy(k, side).wait_send()
            gp_copy(side).wait_send()
    for g in range(2):
        pair(g).wait_send()
        all_of(rx1, g, 1, nq - 1).wait_send()
        all_of(rx2, g, 2, nz - 1).wait_send()
        all_of(rx3, g, 3, 2 * nq - 1).wait_send()


def write_out(gin_ref, g1_ref, g2_ref, gin_hbm, g1_hbm, g2_hbm, sem):
    pairs = ((gin_ref, gin_hbm), (g1_ref, g1_hbm), (g2_ref, g2_hbm))
    copies = [pltpu.make_async_copy(here, there, sem.at[k]) for k, (here, there) in enumerate(pairs)]
    for copy in copies:
        copy.start()
    for copy in copies:
        copy.wait()


def build(mesh, sizes):
    nx, nzh, ny, nzl = sizes
    nq = nx * ny
    nz = nzh * nzl
    per = TILES // (2 * nq)
    total = mesh.shape["dp"] * mesh.shape["space"] * 2 * HGT * WID
    cfg = (nx, nzh, ny, nzl, float(total) ** -0.5)
    hbm = pl.BlockSpec(memory_space=pltpu.HBM)
    vmem = pl.BlockSpec(memory_space=pltpu.VMEM)
    dma = pltpu.SemaphoreType.DMA

    def per_device(layer_input, pre_act, cotangent, weight_one, weight_two):
        held = [
            pltpu.with_memory_space_constraint(v, pltpu.HBM)
            for v in (layer_input, pre_act, cotangent, weight_one, weight_two)
        ]
        gin, g1, g2 = pl.pallas_call(
            functools.partial(kernel, cfg),
            out_shape=(
                jax.ShapeDtypeStruct(layer_input.shape, BF16),
                jax.ShapeDtypeStruct((USED, CH, CH), F32),
                jax.ShapeDtypeStruct((USED, CH, CH), F32),
            ),
            in_specs=[hbm] * 5,
            out_specs=(vmem, vmem, vmem),
            scratch_shapes=[
                pltpu.VMEM((3, CH, 2, HGT, WID), BF16),
                pltpu.VMEM((2, 3, 3, 3, CH, CH), BF16),
                pltpu.VMEM((2, 2, CH, HGT, WID), BF16),
                pltpu.VMEM((3, 4, CH * HGT, WID), F32),
                pltpu.VMEM((416, PLANE), BF16),
                pltpu.VMEM((192, PLANE), BF16),
                pltpu.VMEM((384, PLANE), BF16),
                pltpu.VMEM((384, PLANE), BF16),
                pltpu.VMEM((2, CH, PLANE), F32),
                pltpu.VMEM((2, 96, 288), BF16),
                pltpu.VMEM((2, CH, PLANE), BF16),
                pltpu.VMEM((2, CH * HGT, WID), F32),
                pltpu.VMEM((2, 288, 128), F32),
                pltpu.VMEM((2, TILES, 8, 128), F32),
                pltpu.VMEM((2, TILES // 2, 8, 128), F32),
                pltpu.VMEM((2, nq, per, 8, 128), F32),
                pltpu.VMEM((2, nz, per, 8, 128), F32),
                pltpu.VMEM((2, 2 * nq, per, 8, 128), F32),
                dma((5,)),
                pltpu.SemaphoreType.REGULAR((1,)),
                pltpu.SemaphoreType.REGULAR((2,)),
                pltpu.SemaphoreType.REGULAR((3,)),
                pltpu.SemaphoreType.REGULAR((1,)),
                dma((2, 2)),
                dma((2, 2)),
                dma((2,)),
                dma((2,)),
                dma((2, 4)),
                dma((2, 4)),
            ],
            compiler_params=pltpu.CompilerParams(
                collective_id=0, has_side_effects=True, vmem_limit_bytes=48 * 1024 * 1024
            ),
        )(*held)
        gin, g1, g2 = pl.pallas_call(
            write_out,
            out_shape=tuple(jax.ShapeDtypeStruct(v.shape, v.dtype) for v in (gin, g1, g2)),
            in_specs=[vmem] * 3,
            out_specs=(hbm,) * 3,
            scratch_shapes=[dma((3,))],
            compiler_params=pltpu.CompilerParams(vmem_limit_bytes=8 * 1024 * 1024),
        )(gin, g1, g2)
        shape = weight_one.shape
        return gin, g1.reshape(shape), g2.reshape(shape)

    split = P("dp", None, "space", None, None)
    return jax.shard_map(
        per_device,
        mesh=mesh,
        in_specs=(split, split, split, P(), P()),
        out_specs=(split, P(), P()),
        check_vma=False,
    )


def solution(mesh):
    nzl = 2
    ny = mesh.shape["space"] // nzl
    nx = 4
    nzh = mesh.shape["dp"] // (2 * nx)
    return build(mesh, (nx, nzh, ny, nzl))
```
